256 devices in a mesh: row: 16 (over z, x_lo), col: 16 (over y, x_hi, core).
Axes of the slice: x: 4 (x_hi: 2, x_lo: 2; x = x_hi * 2 + x_lo), y: 4, z: 8, core: 2. Of those that a mesh axis runs over, the one named last changes fastest.
Arguments:
- fock_matrix: bfloat16 [12288, 12288], P('row', 'col'), as said below
- density: bfloat16 [12288, 12288], P('row', 'col'), as said below
- intersection: bfloat16 [12288, 12288], P('row', 'col'), as said below
- pattern: int32 [96, 96], replicated, may hold values from 0 to 1, as said below
Outputs:
- gradient_panel: bfloat16 [12288, 2048], P('row', 'col')
The draws below stay inside these ranges and needn't reach their ends.
Inputs may be any that keep to these rules, and one draw needn't show every extreme that they name: `pattern`: symmetric, with ones on the diagonal; pattern[i, j] is 1 exactly where the centres of blocks i and j lie within the neighbour cutoff of each other. `fock_matrix`: symmetric; zero in every block (i, j) with pattern[i, j] == 0. `density`: symmetric; zero in every block (i, j) with pattern[i, j] == 0. `intersection`: symmetric; zero in every block (i, j) with pattern[i, j] == 0.
All inputs are finite; a program needn't handle non-finite values.
Results may differ from the reference program's by a relative error of at most 0.023.
Values may be sent and summed in bfloat16 or wider, within the bound.
A program may use at most 128 MiB of HBM per device.

```python
import jax
import jax.numpy as jnp
from jax import lax

BLK = 128
RB_DEV = 6
BOX = 5
NBLK = 96
ORDER = 12288
PANEL = 2048
N_ROW = 16
N_COL = 16


def neighbour_blocks(key):
    centres = jax.random.randint(jax.random.fold_in(key, 11), (NBLK, 3), 0, BOX)
    distance = jnp.abs(centres[:, None, :] - centres[None, :, :])
    wrapped = jnp.minimum(distance, BOX - distance)
    squared = jnp.sum(wrapped * wrapped, axis=-1)
    return (squared <= 2).astype(jnp.int32)


def symmetric_sparse(key, salt):
    matrix_order = NBLK * BLK
    blocks = neighbour_blocks(key).astype(jnp.float32)
    full_mask = jnp.repeat(jnp.repeat(blocks, BLK, axis=0), BLK, axis=1)
    spread = (0.152 * matrix_order) ** (-1.0 / 3.0)
    inner = jax.random.fold_in(key, salt)
    entries = jax.random.uniform(inner, (matrix_order, matrix_order), jnp.float32, -2.44948974 * spread, 2.44948974 * spread)
    return ((entries + entries.T) * 0.5 * full_mask).astype(jnp.bfloat16)


def draw_pattern(key, part):
    return neighbour_blocks(key)


def draw_fock_matrix(key, part):
    return symmetric_sparse(key, 21)


def draw_density(key, part):
    return symmetric_sparse(key, 22)


def draw_intersection(key, part):
    return symmetric_sparse(key, 23)


def setup_inputs(seed: int = 0) -> dict:
    key_list = jax.random.split(jax.random.key(seed), 5)
    fock_matrix = draw_fock_matrix(jax.random.fold_in(key_list[4], 71), 0)
    density = draw_density(jax.random.fold_in(key_list[4], 71), 0)
    intersection = draw_intersection(jax.random.fold_in(key_list[4], 71), 0)
    pattern = draw_pattern(jax.random.fold_in(key_list[4], 71), 0)
    return {"fock_matrix": fock_matrix, "density": density, "intersection": intersection, "pattern": pattern}


def panel_of(matrix):
    return matrix.reshape(ORDER, N_COL, ORDER // N_COL)[:, :, :BLK].reshape(ORDER, PANEL)


def reference(fock_matrix, density, intersection, pattern):
    right_sides = (panel_of(intersection), panel_of(fock_matrix))
    group_rows = RB_DEV * BLK

    def add_group(group_index, accumulated):
        start = (group_index * group_rows).astype(jnp.int32)
        rows_block = lax.dynamic_slice_in_dim(density, start, group_rows, 0)
        terms = []
        for member in right_sides:
            member_rows = lax.dynamic_slice_in_dim(member, start, group_rows, 0)
            product = jnp.dot(rows_block.T, member_rows, preferred_element_type=jnp.float32)
            rounded = lax.optimization_barrier(product.astype(jnp.bfloat16))
            terms.append(rounded.astype(jnp.float32))
        return accumulated + jnp.stack(terms)

    combined = lax.fori_loop(jnp.int32(0), jnp.int32(N_ROW), add_group, jnp.zeros((2, ORDER, PANEL), jnp.float32))
    owned_blocks = pattern[:, :: (NBLK // N_COL)].astype(jnp.float32)
    keep_mask = jnp.repeat(jnp.repeat(owned_blocks, BLK, axis=0), BLK, axis=1)
    filtered = (combined * keep_mask[None]).astype(jnp.bfloat16)
    gradient = jnp.dot(fock_matrix, filtered[0], preferred_element_type=jnp.float32)
    gradient = gradient - jnp.dot(intersection, filtered[1], preferred_element_type=jnp.float32)
    return gradient.astype(jnp.bfloat16)
```

```python
import functools

import jax
import jax.numpy as jnp
from jax import lax
from jax.experimental import pallas as pl
from jax.experimental.pallas import tpu as pltpu
from jax.sharding import PartitionSpec as P

BLK = 128
NB = 6
TILE = NB * BLK
HALF = TILE // 2
NQ = 16
NE = NQ * NB
NZ = 8
NY = 4
PER = 4
SLOTS = NZ * PER
MESH = pl.DeviceIdType.MESH
F32 = jnp.float32
BF16 = jnp.bfloat16

OWN_YP, OWN_YM, OWN_X, OWN_C = 0, 2, 4, 6
FWD = 8
PAIR = 16
N_GATHER = 26


def kernel(
    base_ref, pat_s, pat_v, f_hbm, p_hbm, s_hbm, out_ref, most_ref,
    fv, pv, sv, pt, pan, yd, acc, fin, rbuf, xr, yb, zb, gs, gc, rfar, rnear, tx, xg,
    inv, nxt, tab,
    lsem, g_ss, g_rs, a_ss, a_rs, b_ss, b_rs, c_ss, c_rs, d_ss, d_rs,
):
    row, col = lax.axis_index("row"), lax.axis_index("col")
    z, xl = row // 2, row % 2
    y, xh, core = col // 4, (col // 2) % 2, col % 2

    def at_col(yy, xx, cc):
        return yy * 4 + xx * 2 + cc

    up, down, far = (y + 1) % NY, (y + NY - 1) % NY, (y + 2) % NY
    xo, co = 1 - xh, 1 - core
    d_core = (row, at_col(y, xh, co))
    d_x = (row, at_col(y, xo, core))
    d_yp = (row, at_col(up, xh, core))
    d_ym = (row, at_col(down, xh, core))
    d_zp = (((z + 1) % NZ) * 2 + xl, col)
    d_zm = (((z + NZ - 1) % NZ) * 2 + xl, col)
    d_xl = (z * 2 + (1 - xl), col)

    barrier = pltpu.get_barrier_semaphore()
    partners = (d_core, d_x, d_yp, d_ym, d_zp, d_zm, d_xl)
    for d in partners:
        pl.semaphore_signal(barrier, inc=1, device_id=d, device_id_type=MESH)

    loads = [
        pltpu.make_async_copy(p_hbm, pv, lsem.at[0]),
        pltpu.make_async_copy(f_hbm, fv, lsem.at[1]),
        pltpu.make_async_copy(s_hbm, sv, lsem.at[2]),
    ]
    first = pl.ds(0, BLK)
    own = [
        pltpu.make_async_copy(s_hbm.at[:, first], pan.at[0, 0], lsem.at[3]),
        pltpu.make_async_copy(f_hbm.at[:, first], pan.at[0, 1], lsem.at[4]),
    ]
    for c in own + loads:
        c.start()
    pl.semaphore_wait(barrier, len(partners))

    sent = []

    def copy(src, dst, ss, rs, k, dev):
        return pltpu.make_async_remote_copy(
            src_ref=src, dst_ref=dst, send_sem=ss.at[k], recv_sem=rs.at[k], device_id=dev, device_id_type=MESH
        )

    def send(src, dst, ss, rs, k, dev):
        c = copy(src, dst, ss, rs, k, dev)
        c.start()
        sent.append(c)

    def got(dst, ss, rs, k, dev):
        copy(dst, dst, ss, rs, k, dev).wait_recv()

    top, bottom = pl.ds(0, HALF), pl.ds(HALF, HALF)
    s_side, f_side = 0, 1

    def at(dy, dx, dc):
        return dy * 4 + dx * 2 + dc

    def whole(src, dst, k, dev):
        send(pan.at[src], pan.at[dst], g_ss, g_rs, k, dev)

    def part(src, dst, side, k, dev):
        send(pan.at[src, side], pan.at[dst, side], g_ss, g_rs, k, dev)

    def got_whole(dst, k, dev):
        got(pan.at[dst], g_ss, g_rs, k, dev)

    def got_part(dst, side, k, dev):
        got(pan.at[dst, side], g_ss, g_rs, k, dev)

    def give(dy, dx, k):
        whole(at(dy, dx, 0), at(dy, dx, 1), k, d_core)

    def taken(dy, dx, k):
        got_whole(at(dy, dx, 1), k, d_core)

    own[0].wait()
    own[1].wait()
    whole(0, at(3, 0, 0), OWN_YP, d_yp)
    whole(0, at(1, 0, 0), OWN_YM, d_ym)
    whole(0, at(0, 1, 0), OWN_X, d_x)
    give(0, 0, OWN_C)

    base = base_ref[0]
    nxt[NE + 1] = NE
    nxt[NE] = NE

    def count(e, n):
        keep = pat_s[col * NB + e % NB, (e // NB) * NB]
        v = n - base
        ok = (keep > 0) & (v >= 0) & (v < SLOTS)
        inv[e] = jnp.where(ok, v, SLOTS)
        return n + keep

    lax.fori_loop(0, NE, count, jnp.int32(0))

    def back(t, later):
        e = NE - 1 - t
        keep = pat_s[col * NB + e % NB, (e // NB) * NB]
        now = jnp.where(keep > 0, e, later)
        nxt[e] = now
        return now

    lax.fori_loop(0, NE, back, jnp.int32(NE))

    def walk(n, e):
        now = nxt[e]
        tab[n] = now
        return now + 1

    lax.fori_loop(0, NE, walk, jnp.int32(0))

    pat = (pat_v[...] > 0).astype(F32)
    cols = lax.broadcasted_iota(jnp.int32, (NE, NE), 1)
    pat = jnp.where(cols % NB == 0, pat, 0.0)
    grp = lax.broadcasted_iota(jnp.int32, (NQ, NE), 0)
    grp_row = lax.broadcasted_iota(jnp.int32, (NQ, NE), 1) // NB
    counts = jnp.dot(jnp.where(grp == grp_row, 1.0, 0.0), pat, preferred_element_type=F32)
    most_ref[...] = jnp.broadcast_to(
        jnp.max(jnp.sum(counts, axis=1, keepdims=True), axis=0, keepdims=True), most_ref.shape
    )

    fin[pl.ds(SLOTS, 1)] = jnp.zeros((1, BLK, 2 * BLK), BF16)
    yd[pl.ds(NE, 1)] = jnp.zeros((1, BLK, 2 * BLK), BF16)

    loads[0].wait()

    def turn(i, _):
        cols_i = pl.ds(pl.multiple_of(i * BLK, BLK), BLK)
        pt[cols_i, :] = pv[:, cols_i].T
        return 0

    lax.fori_loop(0, NB, turn, 0)

    def products(dy, dx):
        def one(t, _):
            n = at(dy, dx, t)
            q = at_col((y + dy) % NY, (xh + dx) % 2, (core + t) % 2)
            both = jnp.concatenate([pan[n, 0], pan[n, 1]], axis=1)
            r = jnp.dot(pt[...], both, preferred_element_type=F32).astype(BF16)
            yd[pl.ds(q * NB, NB)] = r.reshape(NB, BLK, 2 * BLK)
            return 0

        lax.fori_loop(0, 2, one, 0)

    def from_near(dx, k_lo, k_hi, k_far, k_give):
        got_whole(at(3, dx, 0), k_lo, d_ym)
        part(at(3, dx, 0), at(2, dx, 0), s_side, k_far, d_yp)
        give(3, dx, k_give)
        got_whole(at(1, dx, 0), k_hi, d_yp)
        part(at(1, dx, 0), at(2, dx, 0), f_side, k_far + 1, d_ym)
        give(1, dx, k_give + 1)

    def from_far(dx, k, k_give):
        got_part(at(2, dx, 0), s_side, k, d_ym)
        part(at(2, dx, 0), at(2, dx, 1), s_side, k_give, d_core)
        got_part(at(2, dx, 0), f_side, k + 1, d_yp)
        part(at(2, dx, 0), at(2, dx, 1), f_side, k_give + 1, d_core)

    def taken_far(dx, k):
        got_part(at(2, dx, 1), s_side, k, d_core)
        got_part(at(2, dx, 1), f_side, k + 1, d_core)

    taken(0, 0, OWN_C)
    products(0, 0)
    from_near(0, OWN_YP, OWN_YM, FWD, PAIR)
    got_whole(at(0, 1, 0), OWN_X, d_x)
    whole(at(0, 1, 0), at(3, 1, 0), FWD + 2, d_yp)
    whole(at(0, 1, 0), at(1, 1, 0), FWD + 3, d_ym)
    give(0, 1, PAIR + 2)
    taken(3, 0, PAIR)
    products(3, 0)
    taken(1, 0, PAIR + 1)
    products(1, 0)
    from_far(0, FWD, PAIR + 3)
    taken(0, 1, PAIR + 2)
    products(0, 1)
    taken_far(0, PAIR + 3)
    products(2, 0)
    from_near(1, FWD + 2, FWD + 3, FWD + 4, PAIR + 5)
    taken(3, 1, PAIR + 5)
    products(3, 1)
    taken(1, 1, PAIR + 6)
    products(1, 1)
    from_far(1, FWD + 4, PAIR + 7)
    taken_far(1, PAIR + 7)
    products(2, 1)

    def pack(s, _):
        acc[pl.ds(s, 1)] = yd[pl.ds(tab[base + s], 1)]
        return 0

    lax.fori_loop(0, SLOTS, pack, 0)

    def ring_at(n):
        return (z + n + 2 * NZ) % NZ

    streams = ((0, 0, 4), (1, 1, 4), (0, 1, 3), (1, 0, 3))

    def slots_of(k, h):
        return pl.ds(k * PER + 2 * h, 2)

    def sem_of(d, h, t):
        return (d * 2 + h) * 4 + t

    for t in range(5):
        for d, h, hops in streams:
            u = t - (4 - hops)
            sign = 1 if d == 0 else -1
            to, frm = (d_zp, d_zm) if d == 0 else (d_zm, d_zp)
            if u >= 1:
                k = slots_of(ring_at(sign * (hops - u)), h)
                i = sem_of(d, h, u - 1)
                got(rbuf.at[i], a_ss, a_rs, i, frm)
                acc[k] = (acc[k].astype(F32) + rbuf[i].astype(F32)).astype(BF16)
            if 0 <= u < hops:
                k = slots_of(ring_at(sign * (hops - u)), h)
                i = sem_of(d, h, u)
                send(acc.at[k], rbuf.at[i], a_ss, a_rs, i, to)

    mine = pl.ds(z * PER, PER)
    send(acc.at[mine], xr, d_ss, d_rs, 0, d_xl)
    got(xr, d_ss, d_rs, 0, d_xl)
    fin[mine] = (acc[mine].astype(F32) + xr[...].astype(F32)).astype(BF16)

    for t in range(5):
        for d, h, hops in streams:
            sign = 1 if d == 0 else -1
            to, frm = (d_zp, d_zm) if d == 0 else (d_zm, d_zp)
            k = slots_of(ring_at(-sign * t), h)
            if 1 <= t <= hops:
                got(fin.at[k], b_ss, b_rs, sem_of(d, h, t - 1), frm)
            if t < hops:
                send(fin.at[k], fin.at[k], b_ss, b_rs, sem_of(d, h, t), to)

    loads[1].wait()
    loads[2].wait()

    def pair(n, dy, dx):
        j = ((y + dy) % NY) * 2 + (xh + dx) % 2
        for c in range(2):
            there = pl.ds(c * BLK, BLK)
            q = 2 * j + (core + c) % 2

            def put(i, _, q=q, there=there):
                blk = fin[inv[q * NB + i]]
                rows = pl.ds(pl.multiple_of(i * BLK, BLK), BLK)
                yb[rows, there] = blk[:, :BLK]
                zb[rows, there] = blk[:, BLK:]
                return 0

            lax.fori_loop(0, NB, put, 0)
        g = jnp.dot(fv[...], yb[...], preferred_element_type=F32)
        g = g - jnp.dot(sv[...], zb[...], preferred_element_type=F32)
        gs[n, 0] = g[:, :BLK].astype(BF16)
        gs[n, 1] = g[:, BLK:].astype(BF16)
        cross(n).start()

    def cross(n):
        return copy(gs.at[n, 1], gc.at[n], c_ss, c_rs, n, d_core)

    def join(n):
        cross(n).wait_recv()
        gs[n, 0] = (gs[n, 0].astype(F32) + gc[n].astype(F32)).astype(BF16)

    def far_pair(t, _):
        pair(t, 2, 1 - t)
        return 0

    def near_pair(t, _):
        pair(2 + t, 1 + 2 * (t % 2), 1 - t // 2)
        return 0

    def own_pair(t, _):
        pair(6 + t, 0, 1 - t)
        return 0

    lax.fori_loop(0, 2, far_pair, 0)
    for n in range(2):
        join(n)
        send(gs.at[n, 0, top], rfar.at[2 * n], d_ss, d_rs, 1 + 2 * n, d_yp)
        send(gs.at[n, 0, bottom], rfar.at[2 * n + 1], d_ss, d_rs, 2 + 2 * n, d_ym)
    lax.fori_loop(0, 4, near_pair, 0)
    for n in range(2):
        k = 2 + 2 * n
        join(k)
        got(rfar.at[2 * n], d_ss, d_rs, 1 + 2 * n, d_ym)
        gs[k, 0, top] = (gs[k, 0, top].astype(F32) + rfar[2 * n].astype(F32)).astype(BF16)
        send(gs.at[k, 0], rnear.at[2 * n], d_ss, d_rs, 5 + 2 * n, d_yp)
        k = k + 1
        join(k)
        got(rfar.at[2 * n + 1], d_ss, d_rs, 2 + 2 * n, d_yp)
        gs[k, 0, bottom] = (gs[k, 0, bottom].astype(F32) + rfar[2 * n + 1].astype(F32)).astype(BF16)
        send(gs.at[k, 0], rnear.at[2 * n + 1], d_ss, d_rs, 6 + 2 * n, d_ym)
    lax.fori_loop(0, 2, own_pair, 0)
    for n in range(2):
        join(6 + n)
        got(rnear.at[2 * n], d_ss, d_rs, 5 + 2 * n, d_ym)
        got(rnear.at[2 * n + 1], d_ss, d_rs, 6 + 2 * n, d_yp)
        total = gs[6 + n, 0].astype(F32) + rnear[2 * n].astype(F32) + rnear[2 * n + 1].astype(F32)
        if n == 0:
            tx[...] = total.astype(BF16)
            send(tx, xg, d_ss, d_rs, 9, d_x)
        else:
            out_ref[...] = total
    got(xg, d_ss, d_rs, 9, d_x)
    out_ref[...] += xg[...].astype(F32)

    for c in sent:
        c.wait_send()
    for n in range(NQ // 2):
        cross(n).wait_send()


def one_pass(base, pattern, fock_matrix, density, intersection):
    vmem, dma = pltpu.VMEM, pltpu.SemaphoreType.DMA
    in_vmem = pl.BlockSpec(memory_space=pltpu.VMEM)
    in_smem = pl.BlockSpec(memory_space=pltpu.SMEM)
    raw = pl.BlockSpec(memory_space=pl.ANY)
    tile = vmem((TILE, TILE), BF16)
    return pl.pallas_call(
        kernel,
        out_shape=(
            jax.ShapeDtypeStruct((TILE, BLK), F32),
            jax.ShapeDtypeStruct((8, BLK), F32),
        ),
        in_specs=[in_smem, in_smem, in_vmem, raw, raw, raw],
        out_specs=(in_vmem, in_vmem),
        scratch_shapes=[
            tile, tile, tile, tile,
            vmem((NQ, 2, TILE, BLK), BF16),
            vmem((NE + 1, BLK, 2 * BLK), BF16),
            vmem((SLOTS, BLK, 2 * BLK), BF16),
            vmem((SLOTS + 1, BLK, 2 * BLK), BF16),
            vmem((16, 2, BLK, 2 * BLK), BF16),
            vmem((PER, BLK, 2 * BLK), BF16),
            vmem((TILE, 2 * BLK), BF16),
            vmem((TILE, 2 * BLK), BF16),
            vmem((NQ // 2, 2, TILE, BLK), BF16),
            vmem((NQ // 2, TILE, BLK), BF16),
            vmem((4, HALF, BLK), BF16),
            vmem((4, TILE, BLK), BF16),
            vmem((TILE, BLK), BF16),
            vmem((TILE, BLK), BF16),
            pltpu.SMEM((NE,), jnp.int32),
            pltpu.SMEM((NE + 2,), jnp.int32),
            pltpu.SMEM((NE,), jnp.int32),
            dma((5,)),
            dma((N_GATHER,)), dma((N_GATHER,)),
            dma((16,)), dma((16,)),
            dma((16,)), dma((16,)),
            dma((8,)), dma((8,)),
            dma((10,)), dma((10,)),
        ],
        compiler_params=pltpu.CompilerParams(
            collective_id=0, has_side_effects=True, vmem_limit_bytes=60 * 1024 * 1024
        ),
        name="panel_pass",
    )(base, pattern, pattern, fock_matrix, density, intersection)


def local(fock_matrix, density, intersection, pattern):
    def run(base):
        return one_pass(base.reshape(1), pattern, fock_matrix, density, intersection)

    total, most = run(jnp.int32(0))
    most = most[0, 0].astype(jnp.int32)

    def more(state):
        return state[0] < most

    def again(state):
        base, total = state
        return base + SLOTS, total + run(base)[0]

    _, total = lax.while_loop(more, again, (jnp.int32(SLOTS), total))
    return total.astype(BF16)


def solution(mesh):
    return jax.shard_map(
        local,
        mesh=mesh,
        in_specs=(P("row", "col"), P("row", "col"), P("row", "col"), P()),
        out_specs=P("row", "col"),
        check_vma=False,
    )
```

```python
import functools

import jax
import jax.numpy as jnp
from jax import lax
from jax.experimental import pallas as pl
from jax.experimental.pallas import tpu as pltpu
from jax.sharding import PartitionSpec as P

BLK = 128
NB = 6
TILE = NB * BLK
HALF = TILE // 2
NQ = 16
NE = NQ * NB
NZ = 8
NY = 4
PER = 4
SLOTS = NZ * PER
MESH = pl.DeviceIdType.MESH
F32 = jnp.float32
BF16 = jnp.bfloat16

OWN_YP, OWN_YM, OWN_X, OWN_C = 0, 1, 2, 3
FWD = 4
PAIR = 10
N_GATHER = 19


def kernel(
    base_ref, pat_hbm, f_hbm, p_hbm, s_hbm, out_ref, most_ref,
    fv, pv, sv, pt, pan, yd0, yd1, acc0, acc1, fin0, fin1, rbuf0, rbuf1, xr0, xr1,
    yb, fy, gs, gc, rfar, rnear, tx, xg,
    pat_s, pat_v, inv, nxt, tab,
    lsem, g_ss, g_rs, a_ss, a_rs, b_ss, b_rs, c_ss, c_rs, d_ss, d_rs, e_ss, e_rs,
):
    yd, acc, fin, rbuf, xr = (yd0, yd1), (acc0, acc1), (fin0, fin1), (rbuf0, rbuf1), (xr0, xr1)
    row, col = lax.axis_index("row"), lax.axis_index("col")
    z, xl = row // 2, row % 2
    y, xh, core = col // 4, (col // 2) % 2, col % 2

    def at_col(yy, xx, cc):
        return yy * 4 + xx * 2 + cc

    up, down, far = (y + 1) % NY, (y + NY - 1) % NY, (y + 2) % NY
    xo, co = 1 - xh, 1 - core
    d_core = (row, at_col(y, xh, co))
    d_x = (row, at_col(y, xo, core))
    d_yp = (row, at_col(up, xh, core))
    d_ym = (row, at_col(down, xh, core))
    d_zp = (((z + 1) % NZ) * 2 + xl, col)
    d_zm = (((z + NZ - 1) % NZ) * 2 + xl, col)
    d_xl = (z * 2 + (1 - xl), col)

    barrier = pltpu.get_barrier_semaphore()
    partners = (d_core, d_x, d_yp, d_ym, d_zp, d_zm, d_xl)
    for d in partners:
        pl.semaphore_signal(barrier, inc=1, device_id=d, device_id_type=MESH)

    loads = [
        pltpu.make_async_copy(p_hbm, pv, lsem.at[0]),
        pltpu.make_async_copy(f_hbm, fv, lsem.at[1]),
        pltpu.make_async_copy(s_hbm, sv, lsem.at[2]),
        pltpu.make_async_copy(pat_hbm, pat_s, lsem.at[5]),
        pltpu.make_async_copy(pat_hbm, pat_v, lsem.at[6]),
    ]
    first = pl.ds(0, BLK)
    own = [
        pltpu.make_async_copy(s_hbm.at[:, first], pan.at[0, 0], lsem.at[3]),
        pltpu.make_async_copy(f_hbm.at[:, first], pan.at[0, 1], lsem.at[4]),
    ]
    for c in own + loads:
        c.start()
    pl.semaphore_wait(barrier, len(partners))

    sent = []

    def copy(src, dst, ss, rs, k, dev):
        return pltpu.make_async_remote_copy(
            src_ref=src, dst_ref=dst, send_sem=ss.at[k], recv_sem=rs.at[k], device_id=dev, device_id_type=MESH
        )

    def send(src, dst, ss, rs, k, dev):
        c = copy(src, dst, ss, rs, k, dev)
        c.start()
        sent.append(c)

    def got(dst, ss, rs, k, dev):
        copy(dst, dst, ss, rs, k, dev).wait_recv()

    top, bottom = pl.ds(0, HALF), pl.ds(HALF, HALF)

    def at(dy, dx, dc):
        return dy * 4 + dx * 2 + dc

    def whole(s, src, dst, k, dev):
        send(pan.at[src, s], pan.at[dst, s], g_ss, g_rs, s * N_GATHER + k, dev)

    def part(s, src, dst, rows, k, dev):
        send(pan.at[src, s, rows], pan.at[dst, s, rows], g_ss, g_rs, s * N_GATHER + k, dev)

    def got_whole(s, dst, k, dev):
        got(pan.at[dst, s], g_ss, g_rs, s * N_GATHER + k, dev)

    def got_part(s, dst, rows, k, dev):
        got(pan.at[dst, s, rows], g_ss, g_rs, s * N_GATHER + k, dev)

    def give(s, dy, dx, k):
        whole(s, at(dy, dx, 0), at(dy, dx, 1), k, d_core)

    def taken(s, dy, dx, k):
        got_whole(s, at(dy, dx, 1), k, d_core)

    def own_y(s):
        whole(s, 0, at(3, 0, 0), OWN_YP, d_yp)
        whole(s, 0, at(1, 0, 0), OWN_YM, d_ym)

    own[0].wait()
    whole(0, 0, at(0, 1, 0), OWN_X, d_x)
    own_y(0)
    give(0, 0, 0, OWN_C)
    own[1].wait()
    whole(1, 0, at(0, 1, 0), OWN_X, d_x)
    give(1, 0, 0, OWN_C)

    base = base_ref[0]
    loads[3].wait()
    loads[4].wait()
    nxt[NE + 1] = NE
    nxt[NE] = NE

    def count(q, n):
        for i in range(NB):
            keep = pat_s[col * NB + i, q * NB]
            v = n - base
            ok = (keep > 0) & (v >= 0) & (v < SLOTS)
            inv[q * NB + i] = jnp.where(ok, v, SLOTS)
            n = n + keep
        return n

    lax.fori_loop(0, NQ, count, jnp.int32(0))

    def back(t, later):
        q = NQ - 1 - t
        for i in reversed(range(NB)):
            later = jnp.where(pat_s[col * NB + i, q * NB] > 0, q * NB + i, later)
            nxt[q * NB + i] = later
        return later

    lax.fori_loop(0, NQ, back, jnp.int32(NE))

    def walk(n, e):
        now = nxt[e]
        tab[n] = now
        return now + 1

    lax.fori_loop(0, NE, walk, jnp.int32(0))

    pat = (pat_v[...] > 0).astype(F32)
    cols = lax.broadcasted_iota(jnp.int32, (NE, NE), 1)
    pat = jnp.where(cols % NB == 0, pat, 0.0)
    grp = lax.broadcasted_iota(jnp.int32, (NQ, NE), 0)
    grp_row = lax.broadcasted_iota(jnp.int32, (NQ, NE), 1) // NB
    counts = jnp.dot(jnp.where(grp == grp_row, 1.0, 0.0), pat, preferred_element_type=F32)
    most_ref[0] = jnp.max(jnp.sum(counts, axis=1, keepdims=True))

    for side in range(2):
        fin[side][pl.ds(SLOTS, 1)] = jnp.zeros((1, BLK, BLK), BF16)
        yd[side][pl.ds(NE, 1)] = jnp.zeros((1, BLK, BLK), BF16)

    loads[0].wait()

    def turn(i, _):
        cols_i = pl.ds(pl.multiple_of(i * BLK, BLK), BLK)
        pt[cols_i, :] = pv[:, cols_i].T
        return 0

    lax.fori_loop(0, NB, turn, 0)

    def products(s, dy, dx):
        n = at(dy, dx, 0)
        both = jnp.concatenate([pan[n, s], pan[n + 1, s]], axis=1)
        r = jnp.dot(pt[...], both, preferred_element_type=F32).astype(BF16)
        for t in range(2):
            q = at_col((y + dy) % NY, (xh + dx) % 2, (core + t) % 2)
            yd[s][pl.ds(q * NB, NB)] = r[:, t * BLK : (t + 1) * BLK].reshape(NB, BLK, BLK)

    def from_near(s, dx, k_lo, k_hi, k_far, k_give):
        got_whole(s, at(3, dx, 0), k_lo, d_ym)
        part(s, at(3, dx, 0), at(2, dx, 0), top, k_far, d_yp)
        give(s, 3, dx, k_give)
        got_whole(s, at(1, dx, 0), k_hi, d_yp)
        part(s, at(1, dx, 0), at(2, dx, 0), bottom, k_far + 1, d_ym)
        give(s, 1, dx, k_give + 1)

    def from_x(s):
        got_whole(s, at(0, 1, 0), OWN_X, d_x)
        whole(s, at(0, 1, 0), at(3, 1, 0), FWD + 2, d_yp)
        whole(s, at(0, 1, 0), at(1, 1, 0), FWD + 3, d_ym)
        give(s, 0, 1, PAIR + 2)

    def from_far(s, dx, k, k_give):
        got_part(s, at(2, dx, 0), top, k, d_ym)
        part(s, at(2, dx, 0), at(2, dx, 1), top, k_give, d_core)
        got_part(s, at(2, dx, 0), bottom, k + 1, d_yp)
        part(s, at(2, dx, 0), at(2, dx, 1), bottom, k_give + 1, d_core)

    def near_0(s):
        from_near(s, 0, OWN_YP, OWN_YM, FWD, PAIR)

    def near_1(s):
        from_near(s, 1, FWD + 2, FWD + 3, FWD + 4, PAIR + 5)

    def far_0(s):
        from_far(s, 0, FWD, PAIR + 3)

    def far_1(s):
        from_far(s, 1, FWD + 4, PAIR + 7)

    def products_own(s):
        taken(s, 0, 0, OWN_C)
        products(s, 0, 0)

    def products_near(s, dx, k):
        taken(s, 3, dx, k)
        products(s, 3, dx)
        taken(s, 1, dx, k + 1)
        products(s, 1, dx)

    def products_x(s):
        taken(s, 0, 1, PAIR + 2)
        products(s, 0, 1)

    def products_far(s, dx, k):
        got_part(s, at(2, dx, 1), top, k, d_core)
        got_part(s, at(2, dx, 1), bottom, k + 1, d_core)
        products(s, 2, dx)

    def pack(s):
        def one(i, _):
            acc[s][pl.ds(i, 1)] = yd[s][pl.ds(tab[base + i], 1)]
            return 0

        lax.fori_loop(0, SLOTS, one, 0)

    def ring_at(n):
        return (z + n + 2 * NZ) % NZ

    streams = tuple((d, p, 4 if d == p // 2 else 3) for p, d in ((0, 0), (2, 1), (1, 0), (3, 1), (2, 0), (0, 1), (3, 0), (1, 1)))
    slot_order = (0, 2, 1, 3)

    def slot_of(k, p):
        return pl.ds(k * PER + p, 1)

    def sem_of(s, d, p, t):
        return s * 32 + (d * PER + p) * 4 + t

    def towards(d):
        return (1, d_zp, d_zm) if d == 0 else (-1, d_zm, d_zp)

    def arrived(s, d, p, u, hops):
        sign, _, frm = towards(d)
        k = slot_of(ring_at(sign * (hops - u)), p)
        i = sem_of(0, d, p, u - 1)
        got(rbuf[s].at[i], a_ss, a_rs, sem_of(s, d, p, u - 1), frm)
        acc[s][k] = (acc[s][k].astype(F32) + rbuf[s][pl.ds(i, 1)].astype(F32)).astype(BF16)

    def ring_sum(s, t):
        for d, p, hops in streams:
            u = t - (4 - hops)
            sign, to, _ = towards(d)
            if u >= 1:
                arrived(s, d, p, u, hops)
            if u >= 0:
                k = ring_at(sign * (hops - u)) * PER + p
                send(acc[s].at[k], rbuf[s].at[sem_of(0, d, p, u)], a_ss, a_rs, sem_of(s, d, p, u), to)

    def last_sum(s):
        for p in slot_order:
            for d in range(2):
                hops = 4 if d == p // 2 else 3
                arrived(s, d, p, hops, hops)
            send(acc[s].at[z * PER + p], xr[s].at[p], e_ss, e_rs, s * PER + p, d_xl)

    def crossed_x(s):
        for p in slot_order:
            got(xr[s].at[p], e_ss, e_rs, s * PER + p, d_xl)
            k = slot_of(z, p)
            fin[s][k] = (acc[s][k].astype(F32) + xr[s][pl.ds(p, 1)].astype(F32)).astype(BF16)
            for d in range(2):
                onward(s, d, p, 0)

    def onward(s, d, p, t):
        sign, to, _ = towards(d)
        k = ring_at(-sign * t) * PER + p
        send(fin[s].at[k], fin[s].at[k], b_ss, b_rs, sem_of(s, d, p, t), to)

    def ring_gather(s, t):
        for d, p, hops in streams:
            if t <= hops:
                sign, _, frm = towards(d)
                k = ring_at(-sign * t) * PER + p
                got(fin[s].at[k], b_ss, b_rs, sem_of(s, d, p, t - 1), frm)
            if t < hops:
                onward(s, d, p, t)

    def chip(n):
        dy = jnp.where(n < 2, 2, jnp.where(n < 6, 1 + 2 * (n % 2), 0))
        dx = jnp.where(n < 2, 1 - n, jnp.where(n < 6, 1 - (n - 2) // 2, 7 - n))
        return ((y + dy) % NY) * 2 + (xh + dx) % 2

    def spread(s, n):
        j = chip(n)
        for c in range(2):
            there = pl.ds(c * BLK, BLK)
            q = 2 * j + (core + c) % 2

            def put(i, _, q=q, there=there):
                rows = pl.ds(pl.multiple_of(i * BLK, BLK), BLK)
                yb[rows, there] = fin[s][inv[q * NB + i]]
                return 0

            lax.fori_loop(0, NB, put, 0)

    def with_y(n, _):
        spread(0, n)
        fy[n] = jnp.dot(fv[...], yb[...], preferred_element_type=F32)
        return 0

    def cross(n):
        return copy(gs.at[n, 1], gc.at[n], c_ss, c_rs, n, d_core)

    def with_z(n, _):
        spread(1, n)
        g = fy[n] - jnp.dot(sv[...], yb[...], preferred_element_type=F32)
        gs[n, 0] = g[:, :BLK].astype(BF16)
        gs[n, 1] = g[:, BLK:].astype(BF16)
        cross(n).start()
        return 0

    products_own(0)
    near_0(0)
    from_x(0)
    products_near(0, 0, PAIR)
    far_0(0)
    products_x(0)
    products_far(0, 0, PAIR + 3)
    near_1(0)
    own_y(1)
    from_x(1)
    products_near(0, 1, PAIR + 5)
    far_1(0)
    products_far(0, 1, PAIR + 7)
    pack(0)
    ring_sum(0, 0)
    products_own(1)
    near_0(1)
    ring_sum(0, 1)
    products_near(1, 0, PAIR)
    near_1(1)
    products_x(1)
    ring_sum(0, 2)
    far_0(1)
    products_near(1, 1, PAIR + 5)
    far_1(1)
    products_far(1, 0, PAIR + 3)
    products_far(1, 1, PAIR + 7)
    ring_sum(0, 3)
    pack(1)
    ring_sum(1, 0)
    last_sum(0)
    ring_sum(1, 1)
    crossed_x(0)
    ring_sum(1, 2)
    ring_gather(0, 1)
    ring_sum(1, 3)
    ring_gather(0, 2)
    last_sum(1)
    ring_gather(0, 3)
    crossed_x(1)
    ring_gather(0, 4)
    loads[1].wait()
    lax.fori_loop(0, 3, with_y, 0)
    ring_gather(1, 1)
    lax.fori_loop(3, 6, with_y, 0)
    ring_gather(1, 2)
    lax.fori_loop(6, 8, with_y, 0)
    ring_gather(1, 3)
    ring_gather(1, 4)
    loads[2].wait()

    def join(n):
        cross(n).wait_recv()
        gs[n, 0] = (gs[n, 0].astype(F32) + gc[n].astype(F32)).astype(BF16)

    lax.fori_loop(0, 2, with_z, 0)
    for n in range(2):
        join(n)
        send(gs.at[n, 0, top], rfar.at[2 * n], d_ss, d_rs, 1 + 2 * n, d_yp)
        send(gs.at[n, 0, bottom], rfar.at[2 * n + 1], d_ss, d_rs, 2 + 2 * n, d_ym)
    lax.fori_loop(2, 6, with_z, 0)
    for n in range(2):
        k = 2 + 2 * n
        join(k)
        got(rfar.at[2 * n], d_ss, d_rs, 1 + 2 * n, d_ym)
        gs[k, 0, top] = (gs[k, 0, top].astype(F32) + rfar[2 * n].astype(F32)).astype(BF16)
        send(gs.at[k, 0], rnear.at[2 * n], d_ss, d_rs, 5 + 2 * n, d_yp)
        k = k + 1
        join(k)
        got(rfar.at[2 * n + 1], d_ss, d_rs, 2 + 2 * n, d_yp)
        gs[k, 0, bottom] = (gs[k, 0, bottom].astype(F32) + rfar[2 * n + 1].astype(F32)).astype(BF16)
        send(gs.at[k, 0], rnear.at[2 * n + 1], d_ss, d_rs, 6 + 2 * n, d_ym)
    lax.fori_loop(6, 8, with_z, 0)
    for n in range(2):
        join(6 + n)
        got(rnear.at[2 * n], d_ss, d_rs, 5 + 2 * n, d_ym)
        got(rnear.at[2 * n + 1], d_ss, d_rs, 6 + 2 * n, d_yp)
        total = gs[6 + n, 0].astype(F32) + rnear[2 * n].astype(F32) + rnear[2 * n + 1].astype(F32)
        if n == 0:
            tx[...] = total.astype(BF16)
            send(tx, xg, d_ss, d_rs, 9, d_x)
        else:
            mine_total = total
    got(xg, d_ss, d_rs, 9, d_x)
    out_ref[...] = (mine_total + xg[...].astype(F32)).astype(BF16)

    for c in sent:
        c.wait_send()
    for n in range(NQ // 2):
        cross(n).wait_send()


def one_pass(base, pattern, fock_matrix, density, intersection):
    vmem, dma = pltpu.VMEM, pltpu.SemaphoreType.DMA
    in_vmem = pl.BlockSpec(memory_space=pltpu.VMEM)
    in_smem = pl.BlockSpec(memory_space=pltpu.SMEM)
    raw = pl.BlockSpec(memory_space=pl.ANY)
    tile = vmem((TILE, TILE), BF16)
    return pl.pallas_call(
        kernel,
        out_shape=(
            jax.ShapeDtypeStruct((TILE, BLK), BF16),
            jax.ShapeDtypeStruct((1,), F32),
        ),
        in_specs=[in_smem, raw, raw, raw, raw],
        out_specs=(in_vmem, in_smem),
        scratch_shapes=[
            tile, tile, tile, tile,
            vmem((NQ, 2, TILE, BLK), BF16),
            *[vmem((NE + 1, BLK, BLK), BF16)] * 2,
            *[vmem((SLOTS, BLK, BLK), BF16)] * 2,
            *[vmem((SLOTS + 1, BLK, BLK), BF16)] * 2,
            *[vmem((32, BLK, BLK), BF16)] * 2,
            *[vmem((PER, BLK, BLK), BF16)] * 2,
            vmem((TILE, 2 * BLK), BF16),
            vmem((NQ // 2, TILE, 2 * BLK), F32),
            vmem((NQ // 2, 2, TILE, BLK), BF16),
            vmem((NQ // 2, TILE, BLK), BF16),
            vmem((4, HALF, BLK), BF16),
            vmem((4, TILE, BLK), BF16),
            vmem((TILE, BLK), BF16),
            vmem((TILE, BLK), BF16),
            pltpu.SMEM((NE, NE), jnp.int32),
            vmem((NE, NE), jnp.int32),
            pltpu.SMEM((NE,), jnp.int32),
            pltpu.SMEM((NE + 2,), jnp.int32),
            pltpu.SMEM((NE,), jnp.int32),
            dma((7,)),
            dma((2 * N_GATHER,)), dma((2 * N_GATHER,)),
            dma((64,)), dma((64,)),
            dma((64,)), dma((64,)),
            dma((8,)), dma((8,)),
            dma((10,)), dma((10,)),
            dma((8,)), dma((8,)),
        ],
        compiler_params=pltpu.CompilerParams(
            collective_id=0, has_side_effects=True, vmem_limit_bytes=60 * 1024 * 1024
        ),
        name="panel_pass",
    )(base, pattern, fock_matrix, density, intersection)


def local(fock_matrix, density, intersection, pattern):
    def run(base):
        return one_pass(base.reshape(1), pattern, fock_matrix, density, intersection)

    first, most = run(jnp.int32(0))

    def more(state):
        return state[0].astype(F32) < most[0]

    def again(state):
        base, total = state
        return base + SLOTS, total + run(base)[0].astype(F32)

    def rest():
        return lax.while_loop(more, again, (jnp.int32(SLOTS), first.astype(F32)))[1].astype(BF16)

    return lax.cond(most[0] > SLOTS, rest, lambda: first)


def solution(mesh):
    return jax.shard_map(
        local,
        mesh=mesh,
        in_specs=(P("row", "col"), P("row", "col"), P("row", "col"), P()),
        out_specs=P("row", "col"),
        check_vma=False,
    )
```

```python
import functools

import jax
import jax.numpy as jnp
from jax import lax
from jax.experimental import pallas as pl
from jax.experimental.pallas import tpu as pltpu
from jax.sharding import PartitionSpec as P

BLK = 128
NB = 6
TILE = NB * BLK
HALF = TILE // 2
NQ = 16
NE = NQ * NB
NZ = 8
NY = 4
PER = 4
SLOTS = NZ * PER
MESH = pl.DeviceIdType.MESH
F32 = jnp.float32
BF16 = jnp.bfloat16

OWN_YP, OWN_YM, OWN_X, OWN_C = 0, 1, 2, 3
FWD = 4
PAIR = 10
N_GATHER = 19


def kernel(
    base_ref, pat_hbm, f_hbm, p_hbm, s_hbm, out_ref, most_ref,
    fv, pv, sv, pt, pan, yd0, yd1, acc0, acc1, fin0, fin1, rbuf0, rbuf1, xr0, xr1,
    yb, fy, gs, gc, rfar, rnear, tx, xg,
    pat_s, pat_v, inv, nxt, tab,
    lsem, g_ss, g_rs, a_ss, a_rs, b_ss, b_rs, c_ss, c_rs, d_ss, d_rs, e_ss, e_rs,
):
    yd, acc, fin, rbuf, xr = (yd0, yd1), (acc0, acc1), (fin0, fin1), (rbuf0, rbuf1), (xr0, xr1)
    row, col = lax.axis_index("row"), lax.axis_index("col")
    z, xl = row // 2, row % 2
    y, xh, core = col // 4, (col // 2) % 2, col % 2

    def at_col(yy, xx, cc):
        return yy * 4 + xx * 2 + cc

    up, down, far = (y + 1) % NY, (y + NY - 1) % NY, (y + 2) % NY
    xo, co = 1 - xh, 1 - core
    d_core = (row, at_col(y, xh, co))
    d_x = (row, at_col(y, xo, core))
    d_yp = (row, at_col(up, xh, core))
    d_ym = (row, at_col(down, xh, core))
    d_zp = (((z + 1) % NZ) * 2 + xl, col)
    d_zm = (((z + NZ - 1) % NZ) * 2 + xl, col)
    d_xl = (z * 2 + (1 - xl), col)

    barrier = pltpu.get_barrier_semaphore()
    partners = (d_core, d_x, d_yp, d_ym, d_zp, d_zm, d_xl)
    for d in partners:
        pl.semaphore_signal(barrier, inc=1, device_id=d, device_id_type=MESH)

    loads = [
        pltpu.make_async_copy(p_hbm, pv, lsem.at[0]),
        pltpu.make_async_copy(f_hbm, fv, lsem.at[1]),
        pltpu.make_async_copy(s_hbm, sv, lsem.at[2]),
        pltpu.make_async_copy(pat_hbm, pat_s, lsem.at[5]),
        pltpu.make_async_copy(pat_hbm, pat_v, lsem.at[6]),
    ]
    first = pl.ds(0, BLK)
    own = [
        pltpu.make_async_copy(s_hbm.at[:, first], pan.at[0, 0], lsem.at[3]),
        pltpu.make_async_copy(f_hbm.at[:, first], pan.at[0, 1], lsem.at[4]),
    ]
    for c in own + loads:
        c.start()
    pl.semaphore_wait(barrier, len(partners))

    sent = []

    def copy(src, dst, ss, rs, k, dev):
        return pltpu.make_async_remote_copy(
            src_ref=src, dst_ref=dst, send_sem=ss.at[k], recv_sem=rs.at[k], device_id=dev, device_id_type=MESH
        )

    def send(src, dst, ss, rs, k, dev):
        c = copy(src, dst, ss, rs, k, dev)
        c.start()
        sent.append(c)

    def got(dst, ss, rs, k, dev):
        copy(dst, dst, ss, rs, k, dev).wait_recv()

    top, bottom = pl.ds(0, HALF), pl.ds(HALF, HALF)

    def at(dy, dx, dc):
        return dy * 4 + dx * 2 + dc

    def whole(s, src, dst, k, dev):
        send(pan.at[src, s], pan.at[dst, s], g_ss, g_rs, s * N_GATHER + k, dev)

    def part(s, src, dst, rows, k, dev):
        send(pan.at[src, s, rows], pan.at[dst, s, rows], g_ss, g_rs, s * N_GATHER + k, dev)

    def got_whole(s, dst, k, dev):
        got(pan.at[dst, s], g_ss, g_rs, s * N_GATHER + k, dev)

    def got_part(s, dst, rows, k, dev):
        got(pan.at[dst, s, rows], g_ss, g_rs, s * N_GATHER + k, dev)

    def give(s, dy, dx, k):
        whole(s, at(dy, dx, 0), at(dy, dx, 1), k, d_core)

    def taken(s, dy, dx, k):
        got_whole(s, at(dy, dx, 1), k, d_core)

    def own_y(s):
        whole(s, 0, at(3, 0, 0), OWN_YP, d_yp)
        whole(s, 0, at(1, 0, 0), OWN_YM, d_ym)

    own[0].wait()
    whole(0, 0, at(0, 1, 0), OWN_X, d_x)
    own_y(0)
    give(0, 0, 0, OWN_C)
    own[1].wait()
    whole(1, 0, at(0, 1, 0), OWN_X, d_x)
    give(1, 0, 0, OWN_C)

    base = base_ref[0]
    loads[3].wait()
    loads[4].wait()
    nxt[NE + 1] = NE
    nxt[NE] = NE

    def count(q, n):
        for i in range(NB):
            keep = pat_s[col * NB + i, q * NB]
            v = n - base
            ok = (keep > 0) & (v >= 0) & (v < SLOTS)
            inv[q * NB + i] = jnp.where(ok, v, SLOTS)
            n = n + keep
        return n

    lax.fori_loop(0, NQ, count, jnp.int32(0))

    def back(t, later):
        q = NQ - 1 - t
        for i in reversed(range(NB)):
            later = jnp.where(pat_s[col * NB + i, q * NB] > 0, q * NB + i, later)
            nxt[q * NB + i] = later
        return later

    lax.fori_loop(0, NQ, back, jnp.int32(NE))

    def walk(n, e):
        now = nxt[e]
        tab[n] = now
        return now + 1

    lax.fori_loop(0, NE, walk, jnp.int32(0))

    pat = (pat_v[...] > 0).astype(F32)
    cols = lax.broadcasted_iota(jnp.int32, (NE, NE), 1)
    pat = jnp.where(cols % NB == 0, pat, 0.0)
    grp = lax.broadcasted_iota(jnp.int32, (NQ, NE), 0)
    grp_row = lax.broadcasted_iota(jnp.int32, (NQ, NE), 1) // NB
    counts = jnp.dot(jnp.where(grp == grp_row, 1.0, 0.0), pat, preferred_element_type=F32)
    most_ref[0] = jnp.max(jnp.sum(counts, axis=1, keepdims=True))

    for side in range(2):
        fin[side][pl.ds(SLOTS, 1)] = jnp.zeros((1, BLK, BLK), BF16)
        yd[side][pl.ds(NE, 1)] = jnp.zeros((1, BLK, BLK), BF16)

    loads[0].wait()

    def turn(i, _):
        cols_i = pl.ds(pl.multiple_of(i * BLK, BLK), BLK)
        pt[cols_i, :] = pv[:, cols_i].T
        return 0

    lax.fori_loop(0, NB, turn, 0)

    def products(s, dy, dx):
        n = at(dy, dx, 0)
        both = jnp.concatenate([pan[n, s], pan[n + 1, s]], axis=1)
        r = jnp.dot(pt[...], both, preferred_element_type=F32).astype(BF16)
        for t in range(2):
            q = at_col((y + dy) % NY, (xh + dx) % 2, (core + t) % 2)
            yd[s][pl.ds(q * NB, NB)] = r[:, t * BLK : (t + 1) * BLK].reshape(NB, BLK, BLK)

    def from_near(s, dx, k_lo, k_hi, k_far, k_give):
        got_whole(s, at(3, dx, 0), k_lo, d_ym)
        part(s, at(3, dx, 0), at(2, dx, 0), top, k_far, d_yp)
        give(s, 3, dx, k_give)
        got_whole(s, at(1, dx, 0), k_hi, d_yp)
        part(s, at(1, dx, 0), at(2, dx, 0), bottom, k_far + 1, d_ym)
        give(s, 1, dx, k_give + 1)

    def from_x(s):
        got_whole(s, at(0, 1, 0), OWN_X, d_x)
        whole(s, at(0, 1, 0), at(3, 1, 0), FWD + 2, d_yp)
        whole(s, at(0, 1, 0), at(1, 1, 0), FWD + 3, d_ym)
        give(s, 0, 1, PAIR + 2)

    def from_far(s, dx, k, k_give):
        got_part(s, at(2, dx, 0), top, k, d_ym)
        part(s, at(2, dx, 0), at(2, dx, 1), top, k_give, d_core)
        got_part(s, at(2, dx, 0), bottom, k + 1, d_yp)
        part(s, at(2, dx, 0), at(2, dx, 1), bottom, k_give + 1, d_core)

    def near_0(s):
        from_near(s, 0, OWN_YP, OWN_YM, FWD, PAIR)

    def near_1(s):
        from_near(s, 1, FWD + 2, FWD + 3, FWD + 4, PAIR + 5)

    def far_0(s):
        from_far(s, 0, FWD, PAIR + 3)

    def far_1(s):
        from_far(s, 1, FWD + 4, PAIR + 7)

    def products_own(s):
        taken(s, 0, 0, OWN_C)
        products(s, 0, 0)

    def products_near(s, dx, k):
        taken(s, 3, dx, k)
        products(s, 3, dx)
        taken(s, 1, dx, k + 1)
        products(s, 1, dx)

    def products_x(s):
        taken(s, 0, 1, PAIR + 2)
        products(s, 0, 1)

    def products_far(s, dx, k):
        got_part(s, at(2, dx, 1), top, k, d_core)
        got_part(s, at(2, dx, 1), bottom, k + 1, d_core)
        products(s, 2, dx)

    def pack(s):
        def one(i, _):
            acc[s][pl.ds(i, 1)] = yd[s][pl.ds(tab[base + i], 1)]
            return 0

        lax.fori_loop(0, SLOTS, one, 0)

    def ring_at(n):
        return (z + n + 2 * NZ) % NZ

    streams = tuple((d, p, 4 if d == p // 2 else 3) for p, d in ((0, 0), (2, 1), (1, 0), (3, 1), (2, 0), (0, 1), (3, 0), (1, 1)))
    slot_order = (0, 2, 1, 3)

    def slot_of(k, p):
        return pl.ds(k * PER + p, 1)

    def sem_of(s, d, p, t):
        return s * 32 + (d * PER + p) * 4 + t

    def towards(d):
        return (1, d_zp, d_zm) if d == 0 else (-1, d_zm, d_zp)

    def arrived(s, d, p, u, hops):
        sign, _, frm = towards(d)
        k = slot_of(ring_at(sign * (hops - u)), p)
        i = sem_of(0, d, p, u - 1)
        got(rbuf[s].at[i], a_ss, a_rs, sem_of(s, d, p, u - 1), frm)
        acc[s][k] = (acc[s][k].astype(F32) + rbuf[s][pl.ds(i, 1)].astype(F32)).astype(BF16)

    def ring_sum(s, t):
        for d, p, hops in streams:
            u = t - (4 - hops)
            sign, to, _ = towards(d)
            if u >= 1:
                arrived(s, d, p, u, hops)
            if u >= 0:
                k = ring_at(sign * (hops - u)) * PER + p
                send(acc[s].at[k], rbuf[s].at[sem_of(0, d, p, u)], a_ss, a_rs, sem_of(s, d, p, u), to)

    def last_sum(s):
        for p in slot_order:
            for d in range(2):
                hops = 4 if d == p // 2 else 3
                arrived(s, d, p, hops, hops)
            send(acc[s].at[z * PER + p], xr[s].at[p], e_ss, e_rs, s * PER + p, d_xl)

    def crossed_x(s):
        for p in slot_order:
            got(xr[s].at[p], e_ss, e_rs, s * PER + p, d_xl)
            k = slot_of(z, p)
            fin[s][k] = (acc[s][k].astype(F32) + xr[s][pl.ds(p, 1)].astype(F32)).astype(BF16)
            for d in range(2):
                onward(s, d, p, 0)

    def onward(s, d, p, t):
        sign, to, _ = towards(d)
        k = ring_at(-sign * t) * PER + p
        send(fin[s].at[k], fin[s].at[k], b_ss, b_rs, sem_of(s, d, p, t), to)

    def ring_gather(s, t):
        for d, p, hops in streams:
            if t <= hops:
                sign, _, frm = towards(d)
                k = ring_at(-sign * t) * PER + p
                got(fin[s].at[k], b_ss, b_rs, sem_of(s, d, p, t - 1), frm)
            if t < hops:
                onward(s, d, p, t)

    def chip(n):
        r = n % 3
        dy = jnp.where(n < 6, jnp.where(r < 2, 2 - r, 3), 0)
        dx = jnp.where(n < 6, 1 - n // 3, 7 - n)
        return ((y + dy) % NY) * 2 + (xh + dx) % 2

    def spread(s, n):
        j = chip(n)
        for c in range(2):
            there = pl.ds(c * BLK, BLK)
            q = 2 * j + (core + c) % 2

            def put(i, _, q=q, there=there):
                rows = pl.ds(pl.multiple_of(i * BLK, BLK), BLK)
                yb[rows, there] = fin[s][inv[q * NB + i]]
                return 0

            lax.fori_loop(0, NB, put, 0)

    def with_y(n, _):
        spread(0, n)
        fy[n] = jnp.dot(fv[...], yb[...], preferred_element_type=F32)
        return 0

    def cross(n):
        return copy(gs.at[n, 1], gc.at[n], c_ss, c_rs, n, d_core)

    def with_z(n, _):
        spread(1, n)
        g = fy[n] - jnp.dot(sv[...], yb[...], preferred_element_type=F32)
        gs[n, 0] = g[:, :BLK].astype(BF16)
        gs[n, 1] = g[:, BLK:].astype(BF16)
        cross(n).start()
        return 0

    products_own(0)
    near_0(0)
    from_x(0)
    products_near(0, 0, PAIR)
    far_0(0)
    products_x(0)
    products_far(0, 0, PAIR + 3)
    near_1(0)
    own_y(1)
    from_x(1)
    products_near(0, 1, PAIR + 5)
    far_1(0)
    products_far(0, 1, PAIR + 7)
    pack(0)
    ring_sum(0, 0)
    products_own(1)
    near_0(1)
    ring_sum(0, 1)
    products_near(1, 0, PAIR)
    near_1(1)
    products_x(1)
    ring_sum(0, 2)
    far_0(1)
    products_near(1, 1, PAIR + 5)
    far_1(1)
    products_far(1, 0, PAIR + 3)
    products_far(1, 1, PAIR + 7)
    ring_sum(0, 3)
    pack(1)
    ring_sum(1, 0)
    last_sum(0)
    ring_sum(1, 1)
    crossed_x(0)
    ring_sum(1, 2)
    ring_gather(0, 1)
    ring_sum(1, 3)
    ring_gather(0, 2)
    last_sum(1)
    ring_gather(0, 3)
    crossed_x(1)
    ring_gather(0, 4)
    loads[1].wait()
    lax.fori_loop(0, 3, with_y, 0)
    ring_gather(1, 1)
    lax.fori_loop(3, 6, with_y, 0)
    ring_gather(1, 2)
    lax.fori_loop(6, 8, with_y, 0)
    ring_gather(1, 3)
    ring_gather(1, 4)
    loads[2].wait()

    def join(n):
        cross(n).wait_recv()
        gs[n, 0] = (gs[n, 0].astype(F32) + gc[n].astype(F32)).astype(BF16)

    def send_far(g):
        join(3 * g)
        send(gs.at[3 * g, 0, top], rfar.at[2 * g], d_ss, d_rs, 1 + 2 * g, d_yp)
        send(gs.at[3 * g, 0, bottom], rfar.at[2 * g + 1], d_ss, d_rs, 2 + 2 * g, d_ym)

    def near_part(g, up_side, rows, k):
        n, there = 3 * g + 2 - up_side, rnear.at[2 * g + 1 - up_side, rows]
        return gs.at[n, 0, rows], there, 5 + 4 * g + k

    def send_near(g, up_side, rows, k):
        src, dst, k = near_part(g, up_side, rows, k)
        send(src, dst, d_ss, d_rs, k, d_yp if up_side else d_ym)

    def got_near(g, up_side, rows, k):
        _, dst, k = near_part(g, up_side, rows, k)
        got(dst, d_ss, d_rs, k, d_ym if up_side else d_yp)

    def send_near_free(g):
        join(3 * g + 1)
        send_near(g, 1, bottom, 0)
        join(3 * g + 2)
        send_near(g, 0, top, 1)

    def send_near_tied(g):
        got(rfar.at[2 * g], d_ss, d_rs, 1 + 2 * g, d_ym)
        n = 3 * g + 1
        gs[n, 0, top] = (gs[n, 0, top].astype(F32) + rfar[2 * g].astype(F32)).astype(BF16)
        send_near(g, 1, top, 2)
        got(rfar.at[2 * g + 1], d_ss, d_rs, 2 + 2 * g, d_yp)
        n = 3 * g + 2
        gs[n, 0, bottom] = (gs[n, 0, bottom].astype(F32) + rfar[2 * g + 1].astype(F32)).astype(BF16)
        send_near(g, 0, bottom, 3)

    def total_of(g):
        for up_side, rows, k in ((1, bottom, 0), (0, top, 1), (1, top, 2), (0, bottom, 3)):
            got_near(g, up_side, rows, k)
        return gs[6 + g, 0].astype(F32) + rnear[2 * g].astype(F32) + rnear[2 * g + 1].astype(F32)

    lax.fori_loop(0, 2, with_z, 0)
    send_far(0)
    lax.fori_loop(2, 4, with_z, 0)
    send_near_free(0)
    lax.fori_loop(4, 6, with_z, 0)
    send_near_tied(0)
    send_far(1)
    send_near_free(1)
    lax.fori_loop(6, 8, with_z, 0)
    join(6)
    tx[...] = total_of(0).astype(BF16)
    send(tx, xg, d_ss, d_rs, 0, d_x)
    send_near_tied(1)
    join(7)
    total = total_of(1)
    got(xg, d_ss, d_rs, 0, d_x)
    out_ref[...] = (total + xg[...].astype(F32)).astype(BF16)

    for c in sent:
        c.wait_send()
    for n in range(NQ // 2):
        cross(n).wait_send()


def one_pass(base, pattern, fock_matrix, density, intersection):
    vmem, dma = pltpu.VMEM, pltpu.SemaphoreType.DMA
    in_vmem = pl.BlockSpec(memory_space=pltpu.VMEM)
    in_smem = pl.BlockSpec(memory_space=pltpu.SMEM)
    raw = pl.BlockSpec(memory_space=pl.ANY)
    tile = vmem((TILE, TILE), BF16)
    return pl.pallas_call(
        kernel,
        out_shape=(
            jax.ShapeDtypeStruct((TILE, BLK), BF16),
            jax.ShapeDtypeStruct((1,), F32),
        ),
        in_specs=[in_smem, raw, raw, raw, raw],
        out_specs=(in_vmem, in_smem),
        scratch_shapes=[
            tile, tile, tile, tile,
            vmem((NQ, 2, TILE, BLK), BF16),
            *[vmem((NE + 1, BLK, BLK), BF16)] * 2,
            *[vmem((SLOTS, BLK, BLK), BF16)] * 2,
            *[vmem((SLOTS + 1, BLK, BLK), BF16)] * 2,
            *[vmem((32, BLK, BLK), BF16)] * 2,
            *[vmem((PER, BLK, BLK), BF16)] * 2,
            vmem((TILE, 2 * BLK), BF16),
            vmem((NQ // 2, TILE, 2 * BLK), F32),
            vmem((NQ // 2, 2, TILE, BLK), BF16),
            vmem((NQ // 2, TILE, BLK), BF16),
            vmem((4, HALF, BLK), BF16),
            vmem((4, TILE, BLK), BF16),
            vmem((TILE, BLK), BF16),
            vmem((TILE, BLK), BF16),
            pltpu.SMEM((NE, NE), jnp.int32),
            vmem((NE, NE), jnp.int32),
            pltpu.SMEM((NE,), jnp.int32),
            pltpu.SMEM((NE + 2,), jnp.int32),
            pltpu.SMEM((NE,), jnp.int32),
            dma((7,)),
            dma((2 * N_GATHER,)), dma((2 * N_GATHER,)),
            dma((64,)), dma((64,)),
            dma((64,)), dma((64,)),
            dma((8,)), dma((8,)),
            dma((13,)), dma((13,)),
            dma((8,)), dma((8,)),
        ],
        compiler_params=pltpu.CompilerParams(
            collective_id=0, has_side_effects=True, vmem_limit_bytes=67043328
        ),
        name="panel_pass",
    )(base, pattern, fock_matrix, density, intersection)


def local(fock_matrix, density, intersection, pattern):
    def run(base):
        return one_pass(base.reshape(1), pattern, fock_matrix, density, intersection)

    first, most = run(jnp.int32(0))

    def more(state):
        return state[0].astype(F32) < most[0]

    def again(state):
        base, total = state
        return base + SLOTS, total + run(base)[0].astype(F32)

    def rest():
        return lax.while_loop(more, again, (jnp.int32(SLOTS), first.astype(F32)))[1].astype(BF16)

    return lax.cond(most[0] > SLOTS, rest, lambda: first)


def solution(mesh):
    return jax.shard_map(
        local,
        mesh=mesh,
        in_specs=(P("row", "col"), P("row", "col"), P("row", "col"), P()),
        out_specs=P("row", "col"),
        check_vma=False,
    )
```

```python
import functools

import jax
import jax.numpy as jnp
from jax import lax
from jax.experimental import pallas as pl
from jax.experimental.pallas import tpu as pltpu
from jax.sharding import PartitionSpec as P

BLK = 128
NB = 6
TILE = NB * BLK
HALF = TILE // 2
NQ = 16
NE = NQ * NB
NZ = 8
NY = 4
PER = 4
SLOTS = NZ * PER
MESH = pl.DeviceIdType.MESH
F32 = jnp.float32
BF16 = jnp.bfloat16

OWN_YP, OWN_YM, OWN_X, OWN_C = 0, 1, 2, 3
FWD = 4
PAIR = 10
N_GATHER = 19


def kernel(
    base_ref, pat_hbm, f_hbm, p_hbm, s_hbm, out_ref, most_ref,
    fv, pv, sv, pt, pan, yd0, yd1, acc0, acc1, fin0, fin1, rbuf0, rbuf1, xr0, xr1,
    yb, fy, gs, gc, rfar, rnear, tx, xg,
    pat_s, pat_v, inv, nxt, tab,
    lsem, g_ss, g_rs, a_ss, a_rs, b_ss, b_rs, c_ss, c_rs, d_ss, d_rs, e_ss, e_rs,
):
    yd, acc, fin, rbuf, xr = (yd0, yd1), (acc0, acc1), (fin0, fin1), (rbuf0, rbuf1), (xr0, xr1)
    row, col = lax.axis_index("row"), lax.axis_index("col")
    z, xl = row // 2, row % 2
    y, xh, core = col // 4, (col // 2) % 2, col % 2

    def at_col(yy, xx, cc):
        return yy * 4 + xx * 2 + cc

    up, down, far = (y + 1) % NY, (y + NY - 1) % NY, (y + 2) % NY
    xo, co = 1 - xh, 1 - core
    d_core = (row, at_col(y, xh, co))
    d_x = (row, at_col(y, xo, core))
    d_yp = (row, at_col(up, xh, core))
    d_ym = (row, at_col(down, xh, core))
    d_zp = (((z + 1) % NZ) * 2 + xl, col)
    d_zm = (((z + NZ - 1) % NZ) * 2 + xl, col)
    d_xl = (z * 2 + (1 - xl), col)

    barrier = pltpu.get_barrier_semaphore()
    partners = (d_core, d_x, d_yp, d_ym, d_zp, d_zm, d_xl)
    for d in partners:
        pl.semaphore_signal(barrier, inc=1, device_id=d, device_id_type=MESH)

    loads = [
        pltpu.make_async_copy(p_hbm, pv, lsem.at[0]),
        pltpu.make_async_copy(f_hbm, fv, lsem.at[1]),
        pltpu.make_async_copy(s_hbm, sv, lsem.at[2]),
        pltpu.make_async_copy(pat_hbm, pat_s, lsem.at[5]),
        pltpu.make_async_copy(pat_hbm, pat_v, lsem.at[6]),
    ]
    first = pl.ds(0, BLK)
    own = [
        pltpu.make_async_copy(s_hbm.at[:, first], pan.at[0, 0], lsem.at[3]),
        pltpu.make_async_copy(f_hbm.at[:, first], pan.at[0, 1], lsem.at[4]),
    ]
    for c in own + loads:
        c.start()
    pl.semaphore_wait(barrier, len(partners))

    sent = []

    def copy(src, dst, ss, rs, k, dev):
        return pltpu.make_async_remote_copy(
            src_ref=src, dst_ref=dst, send_sem=ss.at[k], recv_sem=rs.at[k], device_id=dev, device_id_type=MESH
        )

    def send(src, dst, ss, rs, k, dev):
        c = copy(src, dst, ss, rs, k, dev)
        c.start()
        sent.append(c)

    def got(dst, ss, rs, k, dev):
        copy(dst, dst, ss, rs, k, dev).wait_recv()

    top, bottom = pl.ds(0, HALF), pl.ds(HALF, HALF)

    def at(dy, dx, dc):
        return dy * 4 + dx * 2 + dc

    def whole(s, src, dst, k, dev):
        send(pan.at[src, s], pan.at[dst, s], g_ss, g_rs, s * N_GATHER + k, dev)

    def part(s, src, dst, rows, k, dev):
        send(pan.at[src, s, rows], pan.at[dst, s, rows], g_ss, g_rs, s * N_GATHER + k, dev)

    def got_whole(s, dst, k, dev):
        got(pan.at[dst, s], g_ss, g_rs, s * N_GATHER + k, dev)

    def got_part(s, dst, rows, k, dev):
        got(pan.at[dst, s, rows], g_ss, g_rs, s * N_GATHER + k, dev)

    def give(s, dy, dx, k):
        whole(s, at(dy, dx, 0), at(dy, dx, 1), k, d_core)

    def taken(s, dy, dx, k):
        got_whole(s, at(dy, dx, 1), k, d_core)

    def own_y(s):
        whole(s, 0, at(3, 0, 0), OWN_YP, d_yp)
        whole(s, 0, at(1, 0, 0), OWN_YM, d_ym)

    own[0].wait()
    whole(0, 0, at(0, 1, 0), OWN_X, d_x)
    own_y(0)
    give(0, 0, 0, OWN_C)
    own[1].wait()
    whole(1, 0, at(0, 1, 0), OWN_X, d_x)
    give(1, 0, 0, OWN_C)

    base = base_ref[0]
    loads[3].wait()
    loads[4].wait()
    nxt[NE + 1] = NE
    nxt[NE] = NE

    def count(q, n):
        for i in range(NB):
            keep = pat_s[col * NB + i, q * NB]
            v = n - base
            ok = (keep > 0) & (v >= 0) & (v < SLOTS)
            inv[q * NB + i] = jnp.where(ok, v, SLOTS)
            n = n + keep
        return n

    lax.fori_loop(0, NQ, count, jnp.int32(0))

    def back(t, later):
        q = NQ - 1 - t
        for i in reversed(range(NB)):
            later = jnp.where(pat_s[col * NB + i, q * NB] > 0, q * NB + i, later)
            nxt[q * NB + i] = later
        return later

    lax.fori_loop(0, NQ, back, jnp.int32(NE))

    def walk(n, e):
        now = nxt[e]
        tab[n] = now
        return now + 1

    lax.fori_loop(0, NE, walk, jnp.int32(0))

    pat = (pat_v[...] > 0).astype(F32)
    cols = lax.broadcasted_iota(jnp.int32, (NE, NE), 1)
    pat = jnp.where(cols % NB == 0, pat, 0.0)
    grp = lax.broadcasted_iota(jnp.int32, (NQ, NE), 0)
    grp_row = lax.broadcasted_iota(jnp.int32, (NQ, NE), 1) // NB
    counts = jnp.dot(jnp.where(grp == grp_row, 1.0, 0.0), pat, preferred_element_type=F32)
    most_ref[0] = jnp.max(jnp.sum(counts, axis=1, keepdims=True))

    for side in range(2):
        fin[side][pl.ds(SLOTS, 1)] = jnp.zeros((1, BLK, BLK), BF16)
        yd[side][pl.ds(NE, 1)] = jnp.zeros((1, BLK, BLK), BF16)

    loads[0].wait()

    def turn(i, _):
        cols_i = pl.ds(pl.multiple_of(i * BLK, BLK), BLK)
        pt[cols_i, :] = pv[:, cols_i].T
        return 0

    lax.fori_loop(0, NB, turn, 0)

    def products(s, dy, dx):
        n = at(dy, dx, 0)
        both = jnp.concatenate([pan[n, s], pan[n + 1, s]], axis=1)
        r = jnp.dot(pt[...], both, preferred_element_type=F32).astype(BF16)
        for t in range(2):
            q = at_col((y + dy) % NY, (xh + dx) % 2, (core + t) % 2)
            yd[s][pl.ds(q * NB, NB)] = r[:, t * BLK : (t + 1) * BLK].reshape(NB, BLK, BLK)

    def from_near(s, dx, k_lo, k_hi, k_far, k_give):
        got_whole(s, at(3, dx, 0), k_lo, d_ym)
        part(s, at(3, dx, 0), at(2, dx, 0), top, k_far, d_yp)
        give(s, 3, dx, k_give)
        got_whole(s, at(1, dx, 0), k_hi, d_yp)
        part(s, at(1, dx, 0), at(2, dx, 0), bottom, k_far + 1, d_ym)
        give(s, 1, dx, k_give + 1)

    def from_x(s):
        got_whole(s, at(0, 1, 0), OWN_X, d_x)
        whole(s, at(0, 1, 0), at(3, 1, 0), FWD + 2, d_yp)
        whole(s, at(0, 1, 0), at(1, 1, 0), FWD + 3, d_ym)
        give(s, 0, 1, PAIR + 2)

    def from_far(s, dx, k, k_give):
        got_part(s, at(2, dx, 0), top, k, d_ym)
        part(s, at(2, dx, 0), at(2, dx, 1), top, k_give, d_core)
        got_part(s, at(2, dx, 0), bottom, k + 1, d_yp)
        part(s, at(2, dx, 0), at(2, dx, 1), bottom, k_give + 1, d_core)

    def near_0(s):
        from_near(s, 0, OWN_YP, OWN_YM, FWD, PAIR)

    def near_1(s):
        from_near(s, 1, FWD + 2, FWD + 3, FWD + 4, PAIR + 5)

    def far_0(s):
        from_far(s, 0, FWD, PAIR + 3)

    def far_1(s):
        from_far(s, 1, FWD + 4, PAIR + 7)

    def products_own(s):
        taken(s, 0, 0, OWN_C)
        products(s, 0, 0)

    def products_near(s, dx, k):
        taken(s, 3, dx, k)
        products(s, 3, dx)
        taken(s, 1, dx, k + 1)
        products(s, 1, dx)

    def products_x(s):
        taken(s, 0, 1, PAIR + 2)
        products(s, 0, 1)

    def products_far(s, dx, k):
        got_part(s, at(2, dx, 1), top, k, d_core)
        got_part(s, at(2, dx, 1), bottom, k + 1, d_core)
        products(s, 2, dx)

    def pack(s, chunks):
        for n in chunks:
            for p in range(PER):
                i = ring_at(n) * PER + p
                acc[s][pl.ds(i, 1)] = yd[s][pl.ds(tab[base + i], 1)]

    def ring_at(n):
        return (z + n + 2 * NZ) % NZ

    streams = tuple((d, p, 4 if d == p // 2 else 3) for p, d in ((0, 0), (2, 1), (1, 0), (3, 1), (2, 0), (0, 1), (3, 0), (1, 1)))
    slot_order = (0, 2, 1, 3)

    def slot_of(k, p):
        return pl.ds(k * PER + p, 1)

    def sem_of(s, d, p, t):
        return s * 32 + (d * PER + p) * 4 + t

    def towards(d):
        return (1, d_zp, d_zm) if d == 0 else (-1, d_zm, d_zp)

    def arrived(s, d, p, u, hops):
        sign, _, frm = towards(d)
        k = slot_of(ring_at(sign * (hops - u)), p)
        i = sem_of(0, d, p, u - 1)
        got(rbuf[s].at[i], a_ss, a_rs, sem_of(s, d, p, u - 1), frm)
        acc[s][k] = (acc[s][k].astype(F32) + rbuf[s][pl.ds(i, 1)].astype(F32)).astype(BF16)

    def ring_sum(s, t):
        for d, p, hops in streams:
            u = t - (4 - hops)
            sign, to, _ = towards(d)
            if u >= 1:
                arrived(s, d, p, u, hops)
            if u >= 0:
                k = ring_at(sign * (hops - u)) * PER + p
                send(acc[s].at[k], rbuf[s].at[sem_of(0, d, p, u)], a_ss, a_rs, sem_of(s, d, p, u), to)

    def last_sum(s):
        for p in slot_order:
            for d in range(2):
                hops = 4 if d == p // 2 else 3
                arrived(s, d, p, hops, hops)
            send(acc[s].at[z * PER + p], xr[s].at[p], e_ss, e_rs, s * PER + p, d_xl)

    def crossed_x(s):
        for p in slot_order:
            got(xr[s].at[p], e_ss, e_rs, s * PER + p, d_xl)
            k = slot_of(z, p)
            fin[s][k] = (acc[s][k].astype(F32) + xr[s][pl.ds(p, 1)].astype(F32)).astype(BF16)
            for d in range(2):
                onward(s, d, p, 0)

    def onward(s, d, p, t):
        sign, to, _ = towards(d)
        k = ring_at(-sign * t) * PER + p
        send(fin[s].at[k], fin[s].at[k], b_ss, b_rs, sem_of(s, d, p, t), to)

    def ring_gather(s, t):
        for d, p, hops in streams:
            if t <= hops:
                sign, _, frm = towards(d)
                k = ring_at(-sign * t) * PER + p
                got(fin[s].at[k], b_ss, b_rs, sem_of(s, d, p, t - 1), frm)
            if t < hops:
                onward(s, d, p, t)

    def chip(n):
        r = n % 3
        dy = jnp.where(n < 6, jnp.where(r < 2, 2 - r, 3), 0)
        dx = jnp.where(n < 6, 1 - n // 3, 7 - n)
        return ((y + dy) % NY) * 2 + (xh + dx) % 2

    def spread(s, n):
        j = chip(n)
        for c in range(2):
            there = pl.ds(c * BLK, BLK)
            q = 2 * j + (core + c) % 2

            def put(i, _, q=q, there=there):
                rows = pl.ds(pl.multiple_of(i * BLK, BLK), BLK)
                yb[rows, there] = fin[s][inv[q * NB + i]]
                return 0

            lax.fori_loop(0, NB, put, 0)

    def with_y(n, _):
        spread(0, n)
        fy[n] = jnp.dot(fv[...], yb[...], preferred_element_type=F32)
        return 0

    def cross(n):
        return copy(gs.at[n, 1], gc.at[n], c_ss, c_rs, n, d_core)

    def with_z(n, _):
        spread(1, n)
        g = fy[n] - jnp.dot(sv[...], yb[...], preferred_element_type=F32)
        gs[n, 0] = g[:, :BLK].astype(BF16)
        gs[n, 1] = g[:, BLK:].astype(BF16)
        cross(n).start()
        return 0

    products_own(0)
    near_0(0)
    from_x(0)
    products_near(0, 0, PAIR)
    far_0(0)
    products_x(0)
    products_far(0, 0, PAIR + 3)
    near_1(0)
    own_y(1)
    from_x(1)
    products_near(0, 1, PAIR + 5)
    far_1(0)
    products_far(0, 1, PAIR + 7)
    pack(0, (4,))
    ring_sum(0, 0)
    pack(0, (3, -3, 2, -2, 1, -1, 0))
    products_own(1)
    near_0(1)
    ring_sum(0, 1)
    products_near(1, 0, PAIR)
    near_1(1)
    products_x(1)
    ring_sum(0, 2)
    far_0(1)
    products_near(1, 1, PAIR + 5)
    far_1(1)
    products_far(1, 0, PAIR + 3)
    products_far(1, 1, PAIR + 7)
    ring_sum(0, 3)
    pack(1, (4,))
    ring_sum(1, 0)
    pack(1, (3, -3, 2, -2, 1, -1, 0))
    last_sum(0)
    ring_sum(1, 1)
    crossed_x(0)
    ring_sum(1, 2)
    ring_gather(0, 1)
    ring_sum(1, 3)
    ring_gather(0, 2)
    last_sum(1)
    ring_gather(0, 3)
    crossed_x(1)
    ring_gather(0, 4)
    loads[1].wait()
    lax.fori_loop(0, 3, with_y, 0)
    ring_gather(1, 1)
    lax.fori_loop(3, 6, with_y, 0)
    ring_gather(1, 2)
    lax.fori_loop(6, 8, with_y, 0)
    ring_gather(1, 3)
    ring_gather(1, 4)
    loads[2].wait()

    def join(n):
        cross(n).wait_recv()
        gs[n, 0] = (gs[n, 0].astype(F32) + gc[n].astype(F32)).astype(BF16)

    def send_far(g):
        join(3 * g)
        send(gs.at[3 * g, 0, top], rfar.at[2 * g], d_ss, d_rs, 1 + 2 * g, d_yp)
        send(gs.at[3 * g, 0, bottom], rfar.at[2 * g + 1], d_ss, d_rs, 2 + 2 * g, d_ym)

    def near_part(g, up_side, rows, k):
        n, there = 3 * g + 2 - up_side, rnear.at[2 * g + 1 - up_side, rows]
        return gs.at[n, 0, rows], there, 5 + 4 * g + k

    def send_near(g, up_side, rows, k):
        src, dst, k = near_part(g, up_side, rows, k)
        send(src, dst, d_ss, d_rs, k, d_yp if up_side else d_ym)

    def got_near(g, up_side, rows, k):
        _, dst, k = near_part(g, up_side, rows, k)
        got(dst, d_ss, d_rs, k, d_ym if up_side else d_yp)

    def send_near_free(g):
        join(3 * g + 1)
        send_near(g, 1, bottom, 0)
        join(3 * g + 2)
        send_near(g, 0, top, 1)

    def send_near_tied(g):
        got(rfar.at[2 * g], d_ss, d_rs, 1 + 2 * g, d_ym)
        n = 3 * g + 1
        gs[n, 0, top] = (gs[n, 0, top].astype(F32) + rfar[2 * g].astype(F32)).astype(BF16)
        send_near(g, 1, top, 2)
        got(rfar.at[2 * g + 1], d_ss, d_rs, 2 + 2 * g, d_yp)
        n = 3 * g + 2
        gs[n, 0, bottom] = (gs[n, 0, bottom].astype(F32) + rfar[2 * g + 1].astype(F32)).astype(BF16)
        send_near(g, 0, bottom, 3)

    def total_of(g):
        for up_side, rows, k in ((1, bottom, 0), (0, top, 1), (1, top, 2), (0, bottom, 3)):
            got_near(g, up_side, rows, k)
        return gs[6 + g, 0].astype(F32) + rnear[2 * g].astype(F32) + rnear[2 * g + 1].astype(F32)

    lax.fori_loop(0, 2, with_z, 0)
    send_far(0)
    lax.fori_loop(2, 4, with_z, 0)
    send_near_free(0)
    lax.fori_loop(4, 6, with_z, 0)
    send_near_tied(0)
    send_far(1)
    send_near_free(1)
    lax.fori_loop(6, 8, with_z, 0)
    join(6)
    tx[...] = total_of(0).astype(BF16)
    send(tx, xg, d_ss, d_rs, 0, d_x)
    send_near_tied(1)
    join(7)
    total = total_of(1)
    got(xg, d_ss, d_rs, 0, d_x)
    out_ref[...] = (total + xg[...].astype(F32)).astype(BF16)

    for c in sent:
        c.wait_send()
    for n in range(NQ // 2):
        cross(n).wait_send()


def one_pass(base, pattern, fock_matrix, density, intersection):
    vmem, dma = pltpu.VMEM, pltpu.SemaphoreType.DMA
    in_vmem = pl.BlockSpec(memory_space=pltpu.VMEM)
    in_smem = pl.BlockSpec(memory_space=pltpu.SMEM)
    raw = pl.BlockSpec(memory_space=pl.ANY)
    tile = vmem((TILE, TILE), BF16)
    return pl.pallas_call(
        kernel,
        out_shape=(
            jax.ShapeDtypeStruct((TILE, BLK), BF16),
            jax.ShapeDtypeStruct((1,), F32),
        ),
        in_specs=[in_smem, raw, raw, raw, raw],
        out_specs=(in_vmem, in_smem),
        scratch_shapes=[
            tile, tile, tile, tile,
            vmem((NQ, 2, TILE, BLK), BF16),
            *[vmem((NE + 1, BLK, BLK), BF16)] * 2,
            *[vmem((SLOTS, BLK, BLK), BF16)] * 2,
            *[vmem((SLOTS + 1, BLK, BLK), BF16)] * 2,
            *[vmem((32, BLK, BLK), BF16)] * 2,
            *[vmem((PER, BLK, BLK), BF16)] * 2,
            vmem((TILE, 2 * BLK), BF16),
            vmem((NQ // 2, TILE, 2 * BLK), F32),
            vmem((NQ // 2, 2, TILE, BLK), BF16),
            vmem((NQ // 2, TILE, BLK), BF16),
            vmem((4, HALF, BLK), BF16),
            vmem((4, TILE, BLK), BF16),
            vmem((TILE, BLK), BF16),
            vmem((TILE, BLK), BF16),
            pltpu.SMEM((NE, NE), jnp.int32),
            vmem((NE, NE), jnp.int32),
            pltpu.SMEM((NE,), jnp.int32),
            pltpu.SMEM((NE + 2,), jnp.int32),
            pltpu.SMEM((NE,), jnp.int32),
            dma((7,)),
            dma((2 * N_GATHER,)), dma((2 * N_GATHER,)),
            dma((64,)), dma((64,)),
            dma((64,)), dma((64,)),
            dma((8,)), dma((8,)),
            dma((13,)), dma((13,)),
            dma((8,)), dma((8,)),
        ],
        compiler_params=pltpu.CompilerParams(
            collective_id=0, has_side_effects=True, vmem_limit_bytes=67043328
        ),
        name="panel_pass",
    )(base, pattern, fock_matrix, density, intersection)


def local(fock_matrix, density, intersection, pattern):
    def run(base):
        return one_pass(base.reshape(1), pattern, fock_matrix, density, intersection)

    first, most = run(jnp.int32(0))

    def more(state):
        return state[0].astype(F32) < most[0]

    def again(state):
        base, total = state
        return base + SLOTS, total + run(base)[0].astype(F32)

    def rest():
        return lax.while_loop(more, again, (jnp.int32(SLOTS), first.astype(F32)))[1].astype(BF16)

    return lax.cond(most[0] > SLOTS, rest, lambda: first)


def solution(mesh):
    return jax.shard_map(
        local,
        mesh=mesh,
        in_specs=(P("row", "col"), P("row", "col"), P("row", "col"), P()),
        out_specs=P("row", "col"),
        check_vma=False,
    )
```
